256 devices in a mesh: seq: 32 (over x, y, core), tp: 8 (over z).
Axes of the slice: x: 4, y: 4, z: 8, core: 2. Of those that a mesh axis runs over, the one named last changes fastest.
Arguments:
- hidden: bfloat16 [8192, 1024], P('seq'), may hold values from -6 to 6
- norm1_gain: float32 [1024], replicated, may hold values from 0.25 to 1.75
- w_query: bfloat16 [1024, 1024], P(None, 'tp'), may hold values from -3 to 3
- w_key: bfloat16 [1024, 512], P(None, 'tp'), may hold values from -2 to 2
- w_value: bfloat16 [1024, 512], P(None, 'tp'), may hold values from -0.1875 to 0.1875
- w_out: bfloat16 [1024, 1024], P('tp'), may hold values from -0.1875 to 0.1875
- norm2_gain: float32 [1024], replicated, may hold values from 0.25 to 1.75
- w_gate: bfloat16 [32, 1024, 512], P('seq'), may hold values from -0.1875 to 0.1875
- w_up: bfloat16 [32, 1024, 512], P('seq'), may hold values from -0.1875 to 0.1875
- w_down: bfloat16 [32, 512, 1024], P('seq'), may hold values from -0.25 to 0.25
- cache_in: bfloat16 [288, 256, 8, 128], P('seq', None, 'tp'), may hold values from -48 to 48
- cache_len: int32 [4], replicated, may hold values from 0 to 16384, as said below
- block_table: int32 [288], replicated, may hold values from 0 to 287, each once
- routes: int32 [8192, 8], P(('seq', 'tp')), may hold values from 0 to 31, all different within a row; in each aligned block of 32 rows (0 to 31, 32 to 63, ...) at most 12 rows name the same one
- gate_w: float32 [8192, 8], P(('seq', 'tp')), may hold values from 0.05 to 0.35
Outputs:
- hidden_out: bfloat16 [8192, 1024], P(('seq', 'tp'))
- cache_out: bfloat16 [288, 256, 8, 128], P('seq', None, 'tp')
The draws below stay inside these ranges and needn't reach their ends.
Inputs may be any that keep to these rules, and one draw needn't show every extreme that they name: `cache_len`: some request holds exactly 16384 entries. `block_table`: each pool block appears once; pool block b lies on index b // 9 of seq. `routes`: each row names 8 different experts; among the rows of one device (aligned blocks of 32 rows) no expert is named more than 12 times, a bound that some block reaches.
All inputs are finite; a program needn't handle non-finite values.
Results may differ from the reference program's by a relative error of at most 0.035.
The reference program's roundings to bfloat16 on the way count: a program that leaves them out, or rounds other values in their place, can miss the bound.
Values may be sent and summed in bfloat16 or wider, within the bound.
No kernel may reach another device: no remote copies, remote signals or barrier semaphores. Data moves between devices by JAX's collectives and lax.ppermute only.
A program may use at most 128 MiB of HBM per device.

```python
import math
import jax
import jax.numpy as jnp
import numpy as np
from jax import lax

D = 1024
HD = 64
GROUP = 2
FFN = 512
TOP = 8
STRETCH = 2048
LMAX = 16384
BS = 256
KV_HEADS = 8
HEADS = 16
EXPERTS = 32
TOKENS = 8192
REQS = 4
MAXB = 72
POOL = 288
ROWS = 32
CAP = 12
N_SEQ = 32
N_TP = 8


def draw_w_query(key, part):
    sample = jnp.clip(jax.random.normal(key, (D, HEADS * HD), jnp.float32), -6.0, 6.0) * (2.5 / math.sqrt(D))
    sample = jnp.clip(sample, -3.0, 3.0)
    return sample.astype(jnp.bfloat16)


def draw_w_key(key, part):
    sample = jnp.clip(jax.random.normal(key, (D, KV_HEADS * HD), jnp.float32), -6.0, 6.0) * (1.0 / math.sqrt(D))
    sample = jnp.clip(sample, -2.0, 2.0)
    return sample.astype(jnp.bfloat16)


def draw_cache_in(key, part):
    key_part = jax.random.fold_in(key, 11)
    value_part = jax.random.fold_in(key, 12)
    key_rows = jnp.clip(jax.random.normal(key_part, (POOL, BS, KV_HEADS, HD), jnp.float32), -6.0, 6.0)
    value_rows = jnp.clip(jax.random.normal(value_part, (POOL, BS, KV_HEADS, HD), jnp.float32), -6.0, 6.0)
    return jnp.concatenate([key_rows, value_rows], axis=-1).astype(jnp.bfloat16)


def draw_cache_len(key, part):
    length_part = jax.random.fold_in(key, 21)
    pick_part = jax.random.fold_in(key, 22)
    lengths = jax.random.randint(length_part, (REQS,), 0, LMAX + 1, jnp.int32)
    longest = jax.random.randint(pick_part, (), 0, REQS, jnp.int32)
    return jnp.where(jnp.arange(REQS, dtype=jnp.int32) == longest, LMAX, lengths).astype(jnp.int32)


def block_scale(own_key, extent, pieces, smallest, largest):
    def one(position, shards_of):
        draws = jax.random.uniform(jax.random.fold_in(jax.random.fold_in(own_key, 6), position), (shards_of,), jnp.float32, smallest / len(pieces), largest / len(pieces))
        return jnp.repeat(jnp.exp(draws), extent[position] // shards_of).reshape((-1,) + (1,) * (len(extent) - position - 1))

    loudness = one(*pieces[0])
    for cut in pieces[1:]:
        loudness = loudness * one(*cut)
    return loudness


def shared_out(stream_key, own, number, rows, amount, top, limit, lean):
    ranking = jax.random.permutation(stream_key, amount)
    packed, usual = load_shares(amount, rows * top, limit, lean, True), load_shares(amount, rows * top, limit, lean, False)
    places = jnp.arange(amount)

    def named(sizes, offset_by):
        used = int((sizes > 0).sum())
        fixed = max(1, used // 4)
        moved = fixed + (places - fixed + offset_by * (used - fixed)) % max(1, amount - fixed)
        return jnp.zeros((amount,), jnp.int32).at[ranking[jnp.where(places < fixed, places, moved)]].set(jnp.asarray(sizes, jnp.int32))

    sizes = jnp.where(number % 4 == 0, named(packed, number // 4), named(usual, number - number // 4 - 1))
    mixed = jax.random.permutation(jax.random.fold_in(own, 3), amount)
    donor, sink = mixed[0:amount // 2 * 2:2], mixed[1:amount // 2 * 2:2]
    room = jnp.minimum(sizes[donor] - 1, limit - sizes[sink]) // 2
    room = jnp.where((donor == ranking[0]) | (sink == ranking[0]) | (sizes[sink] == 0), 0, jnp.maximum(room, 0))
    moved = jax.random.randint(jax.random.fold_in(own, 4), (amount // 2,), 0, 1 << 20) % (room + 1)
    sizes = sizes.at[donor].add(-moved).at[sink].add(moved)
    labels = jnp.searchsorted(jnp.cumsum(sizes), jnp.arange(rows * top), side="right").astype(jnp.int32)
    grid = labels.reshape(top, rows).T
    grid = grid[jax.random.permutation(jax.random.fold_in(own, 1), rows)]
    offset_by = jax.random.randint(jax.random.fold_in(own, 2), (rows, 1), 0, top)
    return jnp.take_along_axis(grid, (jnp.arange(top)[None, :] + offset_by) % top, axis=1)


def load_shares(amount, total, bound, lean, full):
    weights = [(1 << 20) // math.isqrt(standing ** lean) + 1 for standing in range(1, amount + 1)]
    largest = bound if full else min(bound, max(-(-total // amount), total * weights[0] // sum(weights)))
    least = 1 if total - largest >= amount - 1 else 0
    given, spare = [largest] + [least] * (amount - 1), total - largest - least * (amount - 1)
    while spare > 0:
        movable = [i for i in range(1, amount) if given[i] < largest] or [i for i in range(1, amount) if given[i] < bound]
        pool, budget = sum([weights[i] for i in movable]), spare
        for i in movable:
            more = min(bound - given[i], max(1, budget * weights[i] // pool), spare)
            given[i] = given[i] + more
            spare = spare - more
    return np.array(given)


def scatter_about(stream_key, extent, width, limit, pieces=(), held_as=jnp.bfloat16):
    array = width * jax.random.normal(stream_key, extent, jnp.float32)
    if pieces:
        array = array * block_scale(stream_key, extent, pieces, -0.22, 0.18)
    return jnp.clip(array, -limit, limit).astype(held_as)


def setup_inputs(seed: int = 0) -> dict:
    arg_keys = jax.random.split(jax.random.key(seed), 16)
    hidden = scatter_about(arg_keys[0], (TOKENS, D), 1.0, 6.0, ((0, 32),))
    norm1_gain = jnp.clip(1.0 + 0.15 * jax.random.normal(arg_keys[1], (D,), jnp.float32), 0.25, 1.75)
    w_query = draw_w_query(jax.random.fold_in(arg_keys[15], 71), 0)
    w_key = draw_w_key(jax.random.fold_in(arg_keys[15], 71), 0)
    w_value = scatter_about(arg_keys[4], (D, KV_HEADS * HD), D ** -0.5, 0.1875, ((1, 8),))
    w_out = scatter_about(arg_keys[5], (HEADS * HD, D), (HEADS * HD) ** -0.5, 0.1875, ((0, 8),))
    norm2_gain = jnp.clip(1.0 + 0.15 * jax.random.normal(arg_keys[6], (D,), jnp.float32), 0.25, 1.75)
    w_gate = scatter_about(arg_keys[7], (EXPERTS, D, FFN), D ** -0.5, 0.1875, ((0, 32),))
    w_up = scatter_about(arg_keys[8], (EXPERTS, D, FFN), D ** -0.5, 0.1875, ((0, 32),))
    w_down = scatter_about(arg_keys[9], (EXPERTS, FFN, D), FFN ** -0.5, 0.25, ((0, 32),))
    cache_in = draw_cache_in(jax.random.fold_in(arg_keys[15], 71), 0)
    cache_len = draw_cache_len(jax.random.fold_in(arg_keys[15], 71), 0)
    block_table = jax.random.permutation(arg_keys[12], POOL).astype(jnp.int32)
    routes_keys = jax.random.split(jax.random.fold_in(arg_keys[13], 1), TOKENS // ROWS)
    routes_turns = jax.random.permutation(jax.random.fold_in(arg_keys[13], 3), TOKENS // ROWS)
    routes = jax.vmap(lambda own, number: shared_out(jax.random.fold_in(arg_keys[13], 2), own, number, ROWS, EXPERTS, TOP, CAP, 2))(routes_keys, routes_turns).reshape((TOKENS, TOP))
    gate_w = jnp.clip(0.05 + 0.29999999 * jax.random.uniform(arg_keys[14], (TOKENS, TOP), jnp.float32) ** block_scale(arg_keys[14], (TOKENS, TOP), ((0, 256),), -0.2, 0.2), 0.05, 0.35)
    return dict(hidden=hidden, norm1_gain=norm1_gain, w_query=w_query, w_key=w_key, w_value=w_value, w_out=w_out, norm2_gain=norm2_gain, w_gate=w_gate, w_up=w_up, w_down=w_down, cache_in=cache_in, cache_len=cache_len, block_table=block_table, routes=routes, gate_w=gate_w)


norm_eps = 1e-05
rope_base = 10000.0
mask_fill = -1e+30

def rms_scale(inputs, gains):
    floats = inputs.astype(jnp.float32)
    mean_square = lax.optimization_barrier(jnp.mean(floats * floats, axis=-1, keepdims=True))
    return (floats * lax.rsqrt(mean_square + norm_eps) * gains).astype(jnp.bfloat16)

def rotate(vectors, positions):
    halfway = vectors.shape[-1] // 2
    counter = jnp.arange(halfway, dtype=jnp.int32).astype(jnp.float32)
    frequency = jnp.exp(counter * (-2.0 * math.log(rope_base) / vectors.shape[-1]))
    angles = positions.astype(jnp.float32)[:, None] * frequency[None, :]
    cosine = jnp.cos(angles)[:, None, :]
    sine_part = jnp.sin(angles)[:, None, :]
    front_half = vectors[..., :halfway]
    back_half = vectors[..., halfway:]
    return jnp.concatenate([front_half * cosine - back_half * sine_part, back_half * cosine + front_half * sine_part], axis=-1)

def attend(operands):
    queries, page, fresh_keys, fresh_values, filled = operands
    span = page.shape[0]
    head_dim = fresh_keys.shape[-1]
    fresh_len = fresh_keys.shape[0]
    all_keys = jnp.concatenate([page[:, :head_dim], fresh_keys], axis=0).astype(jnp.float32)
    all_values = jnp.concatenate([page[:, head_dim:], fresh_values], axis=0).astype(jnp.float32)
    scores = jnp.einsum('chd,kd->chk', queries.astype(jnp.float32), all_keys) * (1.0 / math.sqrt(head_dim))
    old_live = jnp.arange(span, dtype=jnp.int32) < filled
    causal = jnp.arange(fresh_len, dtype=jnp.int32)[None, :] <= jnp.arange(fresh_len, dtype=jnp.int32)[:, None]
    allowed = jnp.concatenate([jnp.broadcast_to(old_live[None, :], (fresh_len, span)), causal], axis=1)[:, None, :]
    scores = jnp.where(allowed, scores, mask_fill)
    peak = lax.optimization_barrier(jnp.max(scores, axis=-1, keepdims=True))
    weights = jnp.where(allowed, jnp.exp(scores - peak), 0.0)
    denom = lax.optimization_barrier(jnp.sum(weights, axis=-1))
    rounded = lax.optimization_barrier(weights.astype(jnp.bfloat16)).astype(jnp.float32)
    mixed = jnp.einsum('chk,kd->chd', rounded, all_values)
    return mixed / denom[..., None]

def take_rows(table_rows, picks):
    return table_rows[picks]

def reference(hidden, norm1_gain, w_query, w_key, w_value, w_out, norm2_gain, w_gate, w_up, w_down, cache_in, cache_len, block_table, routes, gate_w):
    token_ids = jnp.arange(TOKENS, dtype=jnp.int32)
    positions = cache_len[token_ids // STRETCH] + token_ids % STRETCH
    normed = rms_scale(hidden, norm1_gain)
    queries = jnp.dot(normed, w_query, preferred_element_type=jnp.float32).reshape(TOKENS, HEADS, HD)
    queries = rotate(queries, positions).astype(jnp.bfloat16)
    key_rows = jnp.dot(normed, w_key, preferred_element_type=jnp.float32).reshape(TOKENS, KV_HEADS, HD)
    key_rows = rotate(key_rows, positions).astype(jnp.bfloat16)
    value_rows = jnp.dot(normed, w_value, preferred_element_type=jnp.float32).reshape(TOKENS, KV_HEADS, HD).astype(jnp.bfloat16)
    span = MAXB * BS
    pages = cache_in[block_table.reshape(REQS, MAXB)].reshape(REQS, span, KV_HEADS, 2 * HD)
    per_query = queries.reshape(REQS, STRETCH, KV_HEADS, GROUP, HD).transpose(0, 2, 1, 3, 4).reshape(REQS * KV_HEADS, STRETCH, GROUP, HD)
    per_page = pages.transpose(0, 2, 1, 3).reshape(REQS * KV_HEADS, span, 2 * HD)
    per_key = key_rows.reshape(REQS, STRETCH, KV_HEADS, HD).transpose(0, 2, 1, 3).reshape(REQS * KV_HEADS, STRETCH, HD)
    per_value = value_rows.reshape(REQS, STRETCH, KV_HEADS, HD).transpose(0, 2, 1, 3).reshape(REQS * KV_HEADS, STRETCH, HD)
    per_fill = jnp.repeat(cache_len, KV_HEADS)
    mixed = lax.map(attend, (per_query, per_page, per_key, per_value, per_fill))
    attention = mixed.reshape(REQS, KV_HEADS, STRETCH, GROUP, HD).transpose(0, 2, 1, 3, 4).reshape(TOKENS, HEADS * HD).astype(jnp.bfloat16)
    residual = (hidden.astype(jnp.float32) + jnp.dot(attention, w_out, preferred_element_type=jnp.float32)).astype(jnp.bfloat16)
    normed2 = rms_scale(residual, norm2_gain)
    bound_rows = N_SEQ * N_TP * CAP

    def one_expert(totals, expert_id):
        matches = routes == expert_id
        chosen = jnp.any(matches, axis=1)
        weights = lax.optimization_barrier(jnp.sum(jnp.where(matches, gate_w, 0.0), axis=1))
        picks = jnp.nonzero(chosen, size=bound_rows, fill_value=0)[0].astype(jnp.int32)
        usable = jnp.arange(bound_rows, dtype=jnp.int32) < jnp.sum(chosen.astype(jnp.int32))
        inputs = normed2[picks]
        gate_part = jnp.dot(inputs, w_gate[expert_id], preferred_element_type=jnp.float32)
        up_part = jnp.dot(inputs, w_up[expert_id], preferred_element_type=jnp.float32)
        inner = (jax.nn.silu(gate_part) * up_part).astype(jnp.bfloat16)
        output = jnp.dot(inner, w_down[expert_id], preferred_element_type=jnp.float32).astype(jnp.bfloat16)
        term = jnp.where(usable[:, None], weights[picks][:, None] * output.astype(jnp.float32), 0.0)
        return (totals.at[picks].add(term), None)
    moe_total, unused = lax.scan(one_expert, jnp.zeros((TOKENS, D), jnp.float32), jnp.arange(EXPERTS, dtype=jnp.int32))
    hidden_out = (residual.astype(jnp.float32) + moe_total).astype(jnp.bfloat16)
    fresh_rows = jnp.concatenate([key_rows, value_rows], axis=-1).reshape(REQS, STRETCH, KV_HEADS, 2 * HD)
    place = jnp.arange(span, dtype=jnp.int32)[None, :]
    filled = cache_len[:, None]
    inside = (place >= filled) & (place < filled + STRETCH)
    source = jnp.clip(place - filled, 0, STRETCH - 1).astype(jnp.int32)
    fresh = jax.vmap(take_rows)(fresh_rows, source)
    merged = jnp.where(inside[:, :, None, None], fresh, pages).reshape(POOL, BS, KV_HEADS, 2 * HD)
    cache_out = jnp.zeros_like(cache_in).at[block_table].set(merged)
    return (hidden_out, cache_out)
```

```python
import functools
import math

import jax
import jax.numpy as jnp
from jax import lax
from jax.experimental import pallas as pl
from jax.experimental.pallas import tpu as pltpu
from jax.sharding import PartitionSpec as P

D = 1024
HD = 64
GROUP = 2
FFN = 512
TOP = 8
STRETCH = 2048
BS = 256
TOK = 256
MAXB = 72
NB = 9
TILES = 8
ROWS = 32
SLOTS = 16
PACK = 72

EPS = 1e-05
ROPE_BASE = 10000.0
LOW = -1e30
LOG2E = 1.4426950408889634
F32 = jnp.float32
BF16 = jnp.bfloat16

VM = pl.BlockSpec(memory_space=pltpu.VMEM)
SM = pl.BlockSpec(memory_space=pltpu.SMEM)


def rms(x, gain):
    mean_square = jnp.mean(x * x, axis=-1, keepdims=True)
    return (x * lax.rsqrt(mean_square + EPS) * gain).astype(BF16)


def spin(rows, cosine, sine):
    front, back = rows[:32], rows[32:]
    return jnp.concatenate([front * cosine - back * sine, back * cosine + front * sine], axis=0)


def project_kernel(hidden, gain, wq, wk, wv, cosine, sine, q_out, rows_out):
    normed = rms(hidden[...].astype(F32), gain[...])
    q = jnp.dot(normed, wq[...], preferred_element_type=F32)
    k = jnp.dot(normed, wk[...], preferred_element_type=F32)
    v = jnp.dot(normed, wv[...], preferred_element_type=F32)
    cos, sin = cosine[...], sine[...]
    qt = q.T
    scale = LOG2E / math.sqrt(HD)
    first = (spin(qt[:64], cos, sin) * scale).astype(BF16)
    second = (spin(qt[64:], cos, sin) * scale).astype(BF16)
    for chip in range(16):
        q_out[2 * chip] = first
        q_out[2 * chip + 1] = second
    kvt = jnp.concatenate([k, v], axis=1).T
    kvt = jnp.concatenate([spin(kvt[:64], cos, sin), kvt[64:]], axis=0)
    rows_out[...] = kvt.T.astype(BF16)


def attend_kernel(meta, q, own, other, new_own, new_other, out, pool, acc, peak, vt):
    pool[0:NB] = own[...]
    pool[NB : 2 * NB] = other[...]
    pool[2 * NB] = new_own[...]
    pool[2 * NB + 1] = new_other[...]
    acc[...] = jnp.zeros_like(acc)
    peak[...] = jnp.full_like(peak, LOW)

    def load(j):
        entries = pool[j]
        turned = entries.astype(F32).T
        ones = (lax.broadcasted_iota(jnp.int32, (8, BS), 0) == 0).astype(F32)
        vt[...] = jnp.concatenate([turned[HD:], ones], axis=0).astype(BF16)
        return entries[:, :HD]

    def step(keys, tile, old, mask):
        scores = jnp.dot(keys, q[tile], preferred_element_type=F32)
        if mask is not None:
            scores = jnp.where(mask, scores, LOW)
        new = jnp.maximum(old, jnp.max(scores, axis=0, keepdims=True))
        weights = jnp.exp2(scores - new).astype(BF16)
        keep = jnp.exp2(old - new)
        mixed = jnp.dot(vt[...], weights, preferred_element_type=F32)
        acc[tile] = acc[tile] * keep + mixed
        return new

    def block(j, carry):
        request = meta[0, j]
        seen = meta[1, j]

        @pl.when(seen >= BS)
        def _():
            keys = load(j)
            olds = peak[request]
            news = []
            for t in range(TILES):
                news.append(step(keys, request * TILES + t, olds[t : t + 1], None))
            peak[request] = jnp.concatenate(news, axis=0)

        @pl.when((seen > 0) & (seen < BS))
        def _():
            keys = load(j)
            mask = lax.broadcasted_iota(jnp.int32, (BS, TOK), 0) < seen
            olds = peak[request]
            news = []
            for t in range(TILES):
                news.append(step(keys, request * TILES + t, olds[t : t + 1], mask))
            peak[request] = jnp.concatenate(news, axis=0)

        return carry

    lax.fori_loop(0, 2 * NB, block, 0)
    request = meta[3, 0]
    gap = lax.broadcasted_iota(jnp.int32, (BS, TOK), 0) - lax.broadcasted_iota(
        jnp.int32, (BS, TOK), 1
    )

    def fresh(k, carry):
        tile = meta[3, 1 + k]
        keys = load(2 * NB + k)

        def visit(t, carry):
            mask = gap <= (t - tile) * TOK
            old = peak[request, pl.ds(t, 1), :]
            new = step(keys, request * TILES + t, old, mask)
            peak[request, pl.ds(t, 1), :] = new
            return carry

        return lax.fori_loop(tile, TILES, visit, carry)

    lax.fori_loop(0, 2, fresh, 0)

    for r in range(4):
        peaks = peak[r]
        for t in range(TILES):
            state = acc[r * TILES + t]
            mass = state[HD : HD + 1]
            some = mass > 0.0
            safe = jnp.where(some, mass, 1.0)
            level = jnp.where(some, peaks[t : t + 1] + jnp.log2(safe), LOW)
            high = level.astype(BF16)
            rest = level - high.astype(F32)
            middle = rest.astype(BF16)
            low = (rest - middle.astype(F32)).astype(BF16)
            share = (state[:HD] * (1.0 / safe)).astype(BF16)
            tail = jnp.concatenate(
                [high.astype(F32), middle.astype(F32), low.astype(F32), jnp.zeros((5, TOK), F32)],
                axis=0,
            ).astype(BF16)
            out[r * TILES + t, 0:HD] = share
            out[r * TILES + t, HD:PACK] = tail


def merge_kernel(parts, w_out, out):
    heads = []
    for h in range(GROUP):
        levels = []
        for i in range(16):
            tail = parts[2 * i + h, HD:PACK].astype(F32)
            levels.append(tail[0:1] + tail[1:2] + tail[2:3])
        top = functools.reduce(jnp.maximum, levels)
        total = jnp.zeros((1, TOK), F32)
        mixed = jnp.zeros((HD, TOK), F32)
        for i in range(16):
            share = jnp.exp2(levels[i] - top)
            total = total + share
            mixed = mixed + parts[2 * i + h, 0:HD].astype(F32) * share
        heads.append(mixed / total)
    attention = jnp.concatenate(heads, axis=0).T.astype(BF16)
    out[...] = jnp.dot(attention, w_out[...], preferred_element_type=F32).astype(BF16)


def one_if(cond):
    return jnp.where(cond, 1.0, 0.0).astype(BF16)


def dispatch_kernel(parts, hidden, gain, routes, send_out, residual_out, rank_out):
    total = parts[0].astype(F32)
    for z in range(1, 8):
        total = total + parts[z].astype(F32)
    residual = (hidden[...].astype(F32) + total).astype(BF16)
    residual_out[...] = residual
    normed = rms(residual.astype(F32), gain[...])
    experts = lax.broadcasted_iota(jnp.int32, (ROWS, 32), 1)
    member = jnp.zeros((ROWS, 32), F32)
    for k in range(TOP):
        member = member + jnp.where(routes[:, k : k + 1] == experts, 1.0, 0.0)
    before = one_if(
        lax.broadcasted_iota(jnp.int32, (ROWS, ROWS), 1)
        < lax.broadcasted_iota(jnp.int32, (ROWS, ROWS), 0)
    )
    rank = jnp.dot(before, member.astype(BF16), preferred_element_type=F32)
    rank = jnp.where(member > 0.0, rank, -1.0)
    rank_out[...] = rank
    slot_rows = lax.broadcasted_iota(jnp.int32, (32 * SLOTS, 32), 0)
    expand = one_if(slot_rows // SLOTS == lax.broadcasted_iota(jnp.int32, (32 * SLOTS, 32), 1))
    spread = lax.dot_general(
        expand, rank.astype(BF16), (((1,), (1,)), ((), ())), preferred_element_type=F32
    )
    pick = one_if(spread == (slot_rows % SLOTS).astype(F32))
    send_out[...] = jnp.dot(pick, normed, preferred_element_type=F32).astype(BF16)


def expert_kernel(rows, w_gate, w_up, w_down, out):
    x = rows[...]
    gate = jnp.dot(x, w_gate[...], preferred_element_type=F32)
    up = jnp.dot(x, w_up[...], preferred_element_type=F32)
    inner = (gate * (1.0 / (1.0 + jnp.exp(-gate))) * up).astype(BF16)
    out[...] = jnp.dot(inner, w_down[...], preferred_element_type=F32).astype(BF16)


def settle_kernel(answers, residual, routes, gate_w, rank, out):
    experts = lax.broadcasted_iota(jnp.int32, (ROWS, 32), 1)
    gains = jnp.zeros((ROWS, 32), F32)
    for k in range(TOP):
        gains = gains + jnp.where(routes[:, k : k + 1] == experts, gate_w[:, k : k + 1], 0.0)
    high = gains.astype(BF16).astype(F32)
    middle = (gains - high).astype(BF16).astype(F32)
    low = gains - high - middle
    columns = lax.broadcasted_iota(jnp.int32, (32, 32 * SLOTS), 1)
    expand = one_if(columns // SLOTS == lax.broadcasted_iota(jnp.int32, (32, 32 * SLOTS), 0))
    stack = jnp.concatenate([rank[...], high, middle, low], axis=0).astype(BF16)
    spread = jnp.dot(stack, expand, preferred_element_type=F32)
    chosen = spread[:ROWS] == (columns % SLOTS).astype(F32)
    mix = jnp.concatenate(
        [jnp.where(chosen, spread[ROWS * i : ROWS * (i + 1)], 0.0) for i in (1, 2, 3)], axis=0
    ).astype(BF16)
    sums = jnp.dot(mix, answers[...], preferred_element_type=F32)
    total = sums[:ROWS] + sums[ROWS : 2 * ROWS] + sums[2 * ROWS :]
    out[...] = (residual[...].astype(F32) + total).astype(BF16)


def cache_kernel(meta, cache, rows, out):
    lane = lax.broadcasted_iota(jnp.int32, (BS, 2 * BS), 1)
    line = lax.broadcasted_iota(jnp.int32, (BS, 2 * BS), 0)
    place = lax.broadcasted_iota(jnp.int32, (BS, 2 * HD), 0)

    def block(j, carry):
        shift = meta[2, j]
        out[j] = cache[j]

        @pl.when((shift > -BS) & (shift < STRETCH))
        def _():
            base = (shift + BS) // BS - 1
            turn = shift - base * BS
            start = meta[0, j] * TILES
            left = rows[start + jnp.maximum(base, 0)]
            right = rows[start + jnp.minimum(base + 1, TILES - 1)]
            both = jnp.concatenate([left, right], axis=0)
            pick = one_if(lane == line + turn)
            fresh = jnp.dot(pick, both, preferred_element_type=F32)
            inside = (place + shift >= 0) & (place + shift < STRETCH)
            out[j] = jnp.where(inside, fresh, cache[j].astype(F32)).astype(BF16)

        return carry

    lax.fori_loop(0, NB, block, 0)


def on_device(
    hidden,
    norm1_gain,
    w_query,
    w_key,
    w_value,
    w_out,
    norm2_gain,
    w_gate,
    w_up,
    w_down,
    cache_in,
    cache_len,
    block_table,
    routes,
    gate_w,
):
    seq = lax.axis_index("seq")
    tp = lax.axis_index("tp")
    sds = jax.ShapeDtypeStruct
    swap = [(i, i ^ 1) for i in range(32)]
    cache = cache_in.reshape(NB, BS, 2 * HD)
    cache_other = lax.ppermute(cache, "seq", swap)

    request = seq // TILES
    filled = lax.dynamic_index_in_dim(cache_len, request, 0, keepdims=False)
    positions = filled + (seq % TILES) * TOK + jnp.arange(TOK, dtype=jnp.int32)
    counter = jnp.arange(HD // 2, dtype=jnp.int32).astype(F32)
    frequency = jnp.exp(counter * (-2.0 * math.log(ROPE_BASE) / HD))
    angles = frequency[:, None] * positions.astype(F32)[None, :]
    cosine, sine = jnp.cos(angles), jnp.sin(angles)

    q_send, new_rows = pl.pallas_call(
        project_kernel,
        out_shape=(sds((32, HD, TOK), BF16), sds((TOK, 2 * HD), BF16)),
        in_specs=[VM] * 7,
        out_specs=(VM, VM),
        name="project",
    )(hidden, norm1_gain[None, :], w_query, w_key, w_value, cosine, sine)
    queries = lax.all_to_all(q_send, "seq", 0, 0, tiled=True)
    rows_other = lax.ppermute(new_rows, "seq", swap)

    counts = jnp.arange(2 * NB, dtype=jnp.int32)
    ids = jnp.where(counts < NB, seq * NB + counts, (seq ^ 1) * NB + counts - NB)
    order = jnp.arange(block_table.shape[0], dtype=jnp.int32)
    slot = jnp.sum(jnp.where(block_table[None, :] == ids[:, None], order[None, :], 0), axis=1)
    block_req = slot // MAXB
    pick = block_req[:, None] == jnp.arange(4, dtype=jnp.int32)[None, :]
    block_len = jnp.sum(jnp.where(pick, cache_len[None, :], 0), axis=1)
    block_pos = slot % MAXB * BS
    shift = block_pos - block_len
    own_tile = seq % TILES
    last = jnp.where(
        counts == 0, request, jnp.where(counts == 1, own_tile, own_tile ^ 1)
    )
    meta = jnp.stack([block_req, jnp.clip(-shift, 0, BS), shift, last])

    partial = pl.pallas_call(
        attend_kernel,
        out_shape=sds((32, PACK, TOK), BF16),
        in_specs=[SM] + [VM] * 5,
        out_specs=VM,
        scratch_shapes=[
            pltpu.VMEM((2 * NB + 2, BS, 2 * HD), BF16),
            pltpu.VMEM((32, PACK, TOK), F32),
            pltpu.VMEM((4, TILES, TOK), F32),
            pltpu.VMEM((PACK, BS), BF16),
        ],
        name="attend",
    )(meta, queries, cache, cache_other, new_rows, rows_other)
    parts = lax.all_to_all(partial, "seq", 0, 0, tiled=True)

    projected = pl.pallas_call(
        merge_kernel,
        out_shape=sds((TOK, D), BF16),
        in_specs=[VM, VM],
        out_specs=VM,
        name="merge",
    )(parts, w_out)
    shares = lax.all_to_all(projected.reshape(8, ROWS, D), "tp", 0, 0, tiled=True)

    own_hidden = lax.dynamic_slice_in_dim(hidden, tp * ROWS, ROWS, 0)
    send, residual, rank = pl.pallas_call(
        dispatch_kernel,
        out_shape=(sds((32 * SLOTS, D), BF16), sds((ROWS, D), BF16), sds((ROWS, 32), F32)),
        in_specs=[VM] * 4,
        out_specs=(VM, VM, VM),
        name="dispatch",
    )(shares, own_hidden, norm2_gain[None, :], routes)
    incoming = lax.all_to_all(send.reshape(32, SLOTS, D), "seq", 0, 0, tiled=True)

    answer = pl.pallas_call(
        expert_kernel,
        out_shape=sds((32 * SLOTS, D), BF16),
        in_specs=[VM] * 4,
        out_specs=VM,
        name="experts",
    )(incoming.reshape(32 * SLOTS, D), w_gate[0], w_up[0], w_down[0])
    returned = lax.all_to_all(answer.reshape(32, SLOTS, D), "seq", 0, 0, tiled=True)

    hidden_out = pl.pallas_call(
        settle_kernel,
        out_shape=sds((ROWS, D), BF16),
        in_specs=[VM] * 5,
        out_specs=VM,
        name="settle",
    )(returned.reshape(32 * SLOTS, D), residual, routes, gate_w, rank)

    spread_rows = jnp.broadcast_to(new_rows[None], (32, TOK, 2 * HD))
    all_rows = lax.all_to_all(spread_rows, "seq", 0, 0, tiled=True)
    cache_out = pl.pallas_call(
        cache_kernel,
        out_shape=sds((NB, BS, 2 * HD), BF16),
        in_specs=[SM, VM, VM],
        out_specs=VM,
        name="cache",
    )(meta, cache, all_rows)
    return (hidden_out, cache_out.reshape(NB, BS, 1, 2 * HD))


def solution(mesh):
    placed = (
        P("seq", None),
        P(),
        P(None, "tp"),
        P(None, "tp"),
        P(None, "tp"),
        P("tp", None),
        P(),
        P("seq", None, None),
        P("seq", None, None),
        P("seq", None, None),
        P("seq", None, "tp", None),
        P(),
        P(),
        P(("seq", "tp"), None),
        P(("seq", "tp"), None),
    )
    return jax.shard_map(
        on_device,
        mesh=mesh,
        in_specs=placed,
        out_specs=(P(("seq", "tp"), None), P("seq", None, "tp", None)),
        check_vma=False,
    )
```

```python
import functools
import math

import jax
import jax.numpy as jnp
from jax import lax
from jax.experimental import pallas as pl
from jax.experimental.pallas import tpu as pltpu
from jax.sharding import PartitionSpec as P

D = 1024
HD = 64
GROUP = 2
FFN = 512
TOP = 8
STRETCH = 2048
BS = 256
TOK = 256
MAXB = 72
NB = 9
TILES = 8
ROWS = 32
LINES = 24
PACK = 72
NS = 4

EPS = 1e-05
ROPE_BASE = 10000.0
LOW = -1e30
LOG2E = 1.4426950408889634
F32 = jnp.float32
BF16 = jnp.bfloat16

VM = pl.BlockSpec(memory_space=pltpu.VMEM)
SM = pl.BlockSpec(memory_space=pltpu.SMEM)


def rms(x, gain):
    mean_square = jnp.mean(x * x, axis=-1, keepdims=True)
    return (x * lax.rsqrt(mean_square + EPS) * gain).astype(BF16)


def spin(rows, cosine, sine):
    front, back = rows[:32], rows[32:]
    return jnp.concatenate([front * cosine - back * sine, back * cosine + front * sine], axis=0)


def project_kernel(hidden, gain, wq, wk, wv, cosine, sine, q_out, rows_out):
    normed = rms(hidden[...].astype(F32), gain[...])
    q = jnp.dot(normed, wq[...], preferred_element_type=F32)
    nt = (((1,), (1,)), ((), ()))
    kt = lax.dot_general(wk[...], normed, nt, preferred_element_type=F32)
    vt = lax.dot_general(wv[...], normed, nt, preferred_element_type=F32)
    cos, sin = cosine[...], sine[...]
    qt = q.T
    scale = LOG2E / math.sqrt(HD)
    first = (spin(qt[:64], cos, sin) * scale).astype(BF16)
    second = (spin(qt[64:], cos, sin) * scale).astype(BF16)
    for chip in range(16):
        q_out[2 * chip] = first
        q_out[2 * chip + 1] = second
    rows_out[...] = jnp.concatenate([spin(kt, cos, sin), vt], axis=0).T.astype(BF16)


def attend_kernel(meta, q, own, other, new_own, new_other, out, pool, acc, peak, vt, sbuf):
    pool[0:NB] = own[...]
    pool[NB : 2 * NB] = other[...]
    pool[2 * NB] = new_own[...]
    pool[2 * NB + 1] = new_other[...]
    acc[...] = jnp.zeros_like(acc)
    peak[...] = jnp.full_like(peak, LOW / 2)

    def load(j):
        entries = pool[j]
        turned = entries.astype(F32).T
        ones = (lax.broadcasted_iota(jnp.int32, (8, BS), 0) == 0).astype(F32)
        vt[...] = jnp.concatenate([turned[HD:], ones], axis=0).astype(BF16)
        return entries[:, :HD]

    def score(keys, tile, old, mask, slot):
        scores = jnp.dot(keys, q[tile], preferred_element_type=F32)
        if mask is not None:
            scores = jnp.where(mask, scores, LOW)
        sbuf[slot] = scores
        return jnp.maximum(old, jnp.max(scores, axis=0, keepdims=True))

    def absorb(tile, old, new, slot):
        weights = jnp.exp2(sbuf[slot] - new).astype(BF16)
        keep = jnp.exp2(old - new)
        mixed = jnp.dot(vt[...], weights, preferred_element_type=F32)
        acc[tile] = acc[tile] * keep + mixed

    def sweep(keys, request, mask_of):
        olds = peak[request]
        base = request * TILES
        news = []

        def ahead(t):
            news.append(score(keys, base + t, olds[t : t + 1], mask_of(t), t % NS))

        ahead(0)
        ahead(1)
        for t in range(TILES):
            if t + 2 < TILES:
                ahead(t + 2)
            absorb(base + t, olds[t : t + 1], news[t], t % NS)
        peak[request] = jnp.concatenate(news, axis=0)

    def block(j, carry):
        request = meta[0, j]
        seen = meta[1, j]

        @pl.when(seen >= BS)
        def _():
            sweep(load(j), request, lambda t: None)

        @pl.when((seen > 0) & (seen < BS))
        def _():
            mask = lax.broadcasted_iota(jnp.int32, (BS, TOK), 0) < seen
            sweep(load(j), request, lambda t: mask)

        return carry

    lax.fori_loop(0, 2 * NB, block, 0)
    request = meta[3, 0]

    def fresh(k, carry):
        tile = meta[3, 1 + k]
        gap = lax.broadcasted_iota(jnp.int32, (BS, TOK), 0) - lax.broadcasted_iota(
            jnp.int32, (BS, TOK), 1
        )
        sweep(load(2 * NB + k), request, lambda t: gap <= (t - tile) * TOK)
        return carry

    lax.fori_loop(0, 2, fresh, 0)

    for r in range(4):
        peaks = peak[r]
        for t in range(TILES):
            state = acc[r * TILES + t]
            mass = state[HD : HD + 1]
            some = mass > 0.0
            safe = jnp.where(some, mass, 1.0)
            level = jnp.where(some, peaks[t : t + 1] + jnp.log2(safe), LOW)
            high = level.astype(BF16)
            rest = level - high.astype(F32)
            middle = rest.astype(BF16)
            low = (rest - middle.astype(F32)).astype(BF16)
            share = (state[:HD] * (1.0 / safe)).astype(BF16)
            tail = jnp.concatenate(
                [high.astype(F32), middle.astype(F32), low.astype(F32), jnp.zeros((5, TOK), F32)],
                axis=0,
            ).astype(BF16)
            out[r * TILES + t, 0:HD] = share
            out[r * TILES + t, HD:PACK] = tail


def merge_kernel(parts, w_out, out):
    heads = []
    for h in range(GROUP):
        levels = []
        for i in range(16):
            tail = parts[2 * i + h, HD:PACK].astype(F32)
            levels.append(tail[0:1] + tail[1:2] + tail[2:3])
        top = functools.reduce(jnp.maximum, levels)
        total = jnp.zeros((1, TOK), F32)
        mixed = jnp.zeros((HD, TOK), F32)
        for i in range(16):
            share = jnp.exp2(levels[i] - top)
            total = total + share
            mixed = mixed + parts[2 * i + h, 0:HD].astype(F32) * share
        heads.append(mixed / total)
    attention = jnp.concatenate(heads, axis=0).T.astype(BF16)
    out[...] = jnp.dot(attention, w_out[...], preferred_element_type=F32).astype(BF16)


def one_if(cond):
    return jnp.where(cond, 1.0, 0.0).astype(BF16)


def ranks(routes):
    experts = lax.broadcasted_iota(jnp.int32, (32, ROWS), 0)
    member = jnp.zeros((32, ROWS), F32)
    for k in range(TOP):
        member = member + jnp.where(routes[k : k + 1, :] == experts, 1.0, 0.0)
    before = one_if(
        lax.broadcasted_iota(jnp.int32, (ROWS, ROWS), 0)
        < lax.broadcasted_iota(jnp.int32, (ROWS, ROWS), 1)
    )
    rank = jnp.dot(member.astype(BF16), before, preferred_element_type=F32)
    return jnp.where(member > 0.0, rank, -1.0)


def line_slots(width):
    line = lax.broadcasted_iota(jnp.int32, (32 * LINES, width), 0) % LINES
    tail = line - 16
    slot = jnp.where(line < 16, line % 8, 8 + tail % 4)
    half = jnp.where(line < 16, line // 8, tail // 4)
    return slot.astype(F32), half


def line_experts():
    line = lax.broadcasted_iota(jnp.int32, (32 * LINES, 32), 0) // LINES
    return one_if(line == lax.broadcasted_iota(jnp.int32, (32 * LINES, 32), 1))


def dispatch_kernel(parts, hidden, gain, routes, send_out, residual_out):
    total = parts[0].astype(F32)
    for z in range(1, 8):
        total = total + parts[z].astype(F32)
    residual = (hidden[...].astype(F32) + total).astype(BF16)
    residual_out[...] = residual
    normed = rms(residual.astype(F32), gain[...])
    spread = jnp.dot(line_experts(), ranks(routes).astype(BF16), preferred_element_type=F32)
    slot, half = line_slots(ROWS)
    chosen = spread == slot
    send_out[...] = (
        jnp.dot(one_if(chosen & (half == 0)), normed[:, :512], preferred_element_type=F32)
        + jnp.dot(one_if(chosen & (half == 1)), normed[:, 512:], preferred_element_type=F32)
    ).astype(BF16)


def glu(gate, up):
    return (gate * (1.0 / (1.0 + jnp.exp(-gate))) * up).astype(BF16)


def expert_kernel(rows, w_gate, w_up, w_down, out):
    main = jnp.concatenate(
        [rows[:, 0:8, :].reshape(256, 512), rows[:, 8:16, :].reshape(256, 512)], axis=1
    )
    tail = rows[:, 16:24, :].reshape(256, 512)

    def fold(w):
        low = jnp.dot(tail, w[:512, :], preferred_element_type=F32)
        high = jnp.dot(tail, w[512:, :], preferred_element_type=F32)
        return low + pltpu.roll(high, 252, 0)

    inner = glu(
        jnp.dot(main, w_gate[...], preferred_element_type=F32),
        jnp.dot(main, w_up[...], preferred_element_type=F32),
    )
    answer = jnp.dot(inner, w_down[...], preferred_element_type=F32).astype(BF16)
    out[:, 0:8, :] = answer[:, :512].reshape(32, 8, 512)
    out[:, 8:16, :] = answer[:, 512:].reshape(32, 8, 512)
    inner = glu(fold(w_gate), fold(w_up))
    answer = jnp.dot(inner, w_down[...], preferred_element_type=F32)
    early = lax.broadcasted_iota(jnp.int32, (256, 512), 0) % 8 < 4
    mixed = jnp.where(early, answer[:, :512], pltpu.roll(answer[:, 512:], 4, 0))
    out[:, 16:24, :] = mixed.astype(BF16).reshape(32, 8, 512)


def settle_kernel(answers, residual, routes, gate_w, out):
    experts = lax.broadcasted_iota(jnp.int32, (32, ROWS), 0)
    gains = jnp.zeros((32, ROWS), F32)
    for k in range(TOP):
        gains = gains + jnp.where(routes[k : k + 1, :] == experts, gate_w[k : k + 1, :], 0.0)
    high = gains.astype(BF16).astype(F32)
    middle = (gains - high).astype(BF16).astype(F32)
    low = gains - high - middle
    rank = ranks(routes)
    expand = line_experts()
    places = jnp.dot(
        expand, jnp.concatenate([rank, rank, rank], axis=1).astype(BF16), preferred_element_type=F32
    )
    weights = jnp.dot(
        expand, jnp.concatenate([high, middle, low], axis=1).astype(BF16), preferred_element_type=F32
    )
    slot, half = line_slots(3 * ROWS)
    weights = jnp.where(places == slot, weights, 0.0)
    base = residual[...].astype(F32)
    for h in range(2):
        mix = jnp.where(half == h, weights, 0.0).T.astype(BF16)
        sums = jnp.dot(mix, answers[...], preferred_element_type=F32)
        total = sums[:ROWS] + sums[ROWS : 2 * ROWS] + sums[2 * ROWS :]
        columns = slice(512 * h, 512 * h + 512)
        out[:, columns] = (base[:, columns] + total).astype(BF16)


def cache_kernel(core, meta, cache, near, far, out):
    side = core[0]

    def tile_rows(i):
        return jnp.where(i % 2 == side, near[i // 2].astype(F32), far[i // 2].astype(F32))

    lane = lax.broadcasted_iota(jnp.int32, (BS, 2 * BS), 1)
    line = lax.broadcasted_iota(jnp.int32, (BS, 2 * BS), 0)
    place = lax.broadcasted_iota(jnp.int32, (BS, 2 * HD), 0)

    def block(j, carry):
        shift = meta[2, j]
        out[j] = cache[j]

        @pl.when((shift > -BS) & (shift < STRETCH))
        def _():
            base = (shift + BS) // BS - 1
            turn = shift - base * BS
            start = meta[0, j] * TILES
            left = tile_rows(start + jnp.maximum(base, 0))
            right = tile_rows(start + jnp.minimum(base + 1, TILES - 1))
            both = jnp.concatenate([left, right], axis=0).astype(BF16)
            pick = one_if(lane == line + turn)
            fresh = jnp.dot(pick, both, preferred_element_type=F32)
            inside = (place + shift >= 0) & (place + shift < STRETCH)
            out[j] = jnp.where(inside, fresh, cache[j].astype(F32)).astype(BF16)

        return carry

    lax.fori_loop(0, NB, block, 0)


def on_device(
    hidden,
    norm1_gain,
    w_query,
    w_key,
    w_value,
    w_out,
    norm2_gain,
    w_gate,
    w_up,
    w_down,
    cache_in,
    cache_len,
    block_table,
    routes,
    gate_w,
):
    seq = lax.axis_index("seq")
    tp = lax.axis_index("tp")
    sds = jax.ShapeDtypeStruct
    swap = [(i, i ^ 1) for i in range(32)]
    cache = cache_in.reshape(NB, BS, 2 * HD)
    cache_other = lax.ppermute(cache, "seq", swap)

    request = seq // TILES
    filled = jnp.sum(jnp.where(jnp.arange(4, dtype=jnp.int32) == request, cache_len, 0))
    positions = filled + (seq % TILES) * TOK + jnp.arange(TOK, dtype=jnp.int32)
    counter = jnp.arange(HD // 2, dtype=jnp.int32).astype(F32)
    frequency = jnp.exp(counter * (-2.0 * math.log(ROPE_BASE) / HD))
    angles = frequency[:, None] * positions.astype(F32)[None, :]
    cosine, sine = jnp.cos(angles), jnp.sin(angles)

    q_send, new_rows = pl.pallas_call(
        project_kernel,
        out_shape=(sds((32, HD, TOK), BF16), sds((TOK, 2 * HD), BF16)),
        in_specs=[VM] * 7,
        out_specs=(VM, VM),
        name="project",
    )(hidden, norm1_gain[None, :], w_query, w_key.T, w_value.T, cosine, sine)
    queries = lax.all_to_all(q_send, "seq", 0, 0, tiled=True)
    rows_other = lax.ppermute(new_rows, "seq", swap)
    queries, row_send = lax.optimization_barrier((queries, new_rows))
    row_send = jnp.broadcast_to(row_send[None], (16, TOK, 2 * HD))
    same_core = [[2 * chip + c for chip in range(16)] for c in range(2)]
    rows_near = lax.all_to_all(row_send, "seq", 0, 0, tiled=True, axis_index_groups=same_core)

    counts = jnp.arange(2 * NB, dtype=jnp.int32)
    ids = jnp.where(counts < NB, seq * NB + counts, (seq ^ 1) * NB + counts - NB)
    order = jnp.arange(block_table.shape[0], dtype=jnp.int32)
    slot = jnp.sum(jnp.where(block_table[None, :] == ids[:, None], order[None, :], 0), axis=1)
    block_req = slot // MAXB
    pick = block_req[:, None] == jnp.arange(4, dtype=jnp.int32)[None, :]
    block_len = jnp.sum(jnp.where(pick, cache_len[None, :], 0), axis=1)
    block_pos = slot % MAXB * BS
    shift = block_pos - block_len
    own_tile = seq % TILES
    last = jnp.where(
        counts == 0, request, jnp.where(counts == 1, own_tile, own_tile ^ 1)
    )
    meta = jnp.stack([block_req, jnp.clip(-shift, 0, BS), shift, last])

    partial = pl.pallas_call(
        attend_kernel,
        out_shape=sds((32, PACK, TOK), BF16),
        in_specs=[SM] + [VM] * 5,
        out_specs=VM,
        scratch_shapes=[
            pltpu.VMEM((2 * NB + 2, BS, 2 * HD), BF16),
            pltpu.VMEM((32, PACK, TOK), F32),
            pltpu.VMEM((4, TILES, TOK), F32),
            pltpu.VMEM((PACK, BS), BF16),
            pltpu.VMEM((NS, BS, TOK), F32),
        ],
        name="attend",
    )(meta, queries, cache, cache_other, new_rows, rows_other)
    partial, rows_near = lax.optimization_barrier((partial, rows_near))
    parts = lax.all_to_all(partial, "seq", 0, 0, tiled=True)

    projected = pl.pallas_call(
        merge_kernel,
        out_shape=sds((TOK, D), BF16),
        in_specs=[VM, VM],
        out_specs=VM,
        name="merge",
    )(parts, w_out)
    shares = lax.all_to_all(projected.reshape(8, ROWS, D), "tp", 0, 0, tiled=True)

    own_hidden = lax.dynamic_slice_in_dim(hidden, tp * ROWS, ROWS, 0)
    routes_t, gate_t = routes.T, gate_w.T
    send, residual = pl.pallas_call(
        dispatch_kernel,
        out_shape=(sds((32 * LINES, 512), BF16), sds((ROWS, D), BF16)),
        in_specs=[VM] * 4,
        out_specs=(VM, VM),
        name="dispatch",
    )(shares, own_hidden, norm2_gain[None, :], routes_t)
    incoming = lax.all_to_all(send.reshape(32, LINES, 512), "seq", 0, 0, tiled=True)

    answer = pl.pallas_call(
        expert_kernel,
        out_shape=sds((32, LINES, 512), BF16),
        in_specs=[VM] * 4,
        out_specs=VM,
        name="experts",
    )(incoming, w_gate[0], w_up[0], w_down[0])
    returned = lax.all_to_all(answer, "seq", 0, 0, tiled=True)

    hidden_out = pl.pallas_call(
        settle_kernel,
        out_shape=sds((ROWS, D), BF16),
        in_specs=[VM] * 4,
        out_specs=VM,
        name="settle",
    )(returned.reshape(32 * LINES, 512), residual, routes_t, gate_t)

    rows_far = lax.ppermute(rows_near, "seq", swap)
    core = (seq & 1)[None]
    cache_out = pl.pallas_call(
        cache_kernel,
        out_shape=sds((NB, BS, 2 * HD), BF16),
        in_specs=[SM, SM, VM, VM, VM],
        out_specs=VM,
        name="cache",
    )(core, meta, cache, rows_near, rows_far)
    return (hidden_out, cache_out.reshape(NB, BS, 1, 2 * HD))


def solution(mesh):
    placed = (
        P("seq", None),
        P(),
        P(None, "tp"),
        P(None, "tp"),
        P(None, "tp"),
        P("tp", None),
        P(),
        P("seq", None, None),
        P("seq", None, None),
        P("seq", None, None),
        P("seq", None, "tp", None),
        P(),
        P(),
        P(("seq", "tp"), None),
        P(("seq", "tp"), None),
    )
    return jax.shard_map(
        on_device,
        mesh=mesh,
        in_specs=placed,
        out_specs=(P(("seq", "tp"), None), P("seq", None, "tp", None)),
        check_vma=False,
    )
```

```python
import functools
import math

import jax
import jax.numpy as jnp
from jax import lax
from jax.experimental import pallas as pl
from jax.experimental.pallas import tpu as pltpu
from jax.sharding import PartitionSpec as P

D = 1024
HD = 64
GROUP = 2
FFN = 512
TOP = 8
STRETCH = 2048
BS = 256
TOK = 256
MAXB = 72
NB = 9
TILES = 8
ROWS = 32
LINES = 24
PACK = 72
NS = 4

EPS = 1e-05
ROPE_BASE = 10000.0
LOW = -1e30
LOG2E = 1.4426950408889634
F32 = jnp.float32
BF16 = jnp.bfloat16

VM = pl.BlockSpec(memory_space=pltpu.VMEM)
SM = pl.BlockSpec(memory_space=pltpu.SMEM)
ANY = pl.BlockSpec(memory_space=pl.ANY)
FAR = pl.BlockSpec(memory_space=pltpu.HBM)


def rms(x, gain):
    mean_square = jnp.mean(x * x, axis=-1, keepdims=True)
    return (x * lax.rsqrt(mean_square + EPS) * gain).astype(BF16)


def spin(rows, cosine, sine):
    front, back = rows[:32], rows[32:]
    return jnp.concatenate([front * cosine - back * sine, back * cosine + front * sine], axis=0)


def turns(filled):
    seq = lax.axis_index("seq")
    place = filled[seq // TILES] + (seq % TILES) * TOK
    places = (place + lax.broadcasted_iota(jnp.int32, (HD // 2, TOK), 1)).astype(F32)
    counter = lax.broadcasted_iota(jnp.int32, (HD // 2, TOK), 0).astype(F32)
    angles = places * jnp.exp(counter * (-2.0 * math.log(ROPE_BASE) / HD))
    cycles = jnp.floor(angles * (0.5 / math.pi) + 0.5)
    angles = angles - cycles * 6.28125
    angles = angles - cycles * 0.0019350051879882812
    angles = angles - cycles * 3.0199159819567387e-07
    return jnp.cos(angles), jnp.sin(angles)


def project_kernel(filled, hidden, gain, wq, wk, wv, q_out, rows_out):
    normed = rms(hidden[...].astype(F32), gain[...])
    q = jnp.dot(normed, wq[...], preferred_element_type=F32)
    nt = (((1,), (1,)), ((), ()))
    kt = lax.dot_general(wk[...], normed, nt, preferred_element_type=F32)
    vt = lax.dot_general(wv[...], normed, nt, preferred_element_type=F32)
    cos, sin = turns(filled)
    qt = q.T
    scale = LOG2E / math.sqrt(HD)
    first = (spin(qt[:64], cos, sin) * scale).astype(BF16)
    second = (spin(qt[64:], cos, sin) * scale).astype(BF16)
    for chip in range(16):
        q_out[2 * chip] = first
        q_out[2 * chip + 1] = second
    rows_out[...] = jnp.concatenate([spin(kt, cos, sin), vt], axis=0).T.astype(BF16)


def attend_kernel(
    meta, q, own, other, new_own, new_other, out, pool, acc, peak, vt, sbuf, sems
):
    copies = (
        pltpu.make_async_copy(own, pool.at[0:NB], sems.at[0]),
        pltpu.make_async_copy(other, pool.at[NB : 2 * NB], sems.at[1]),
        pltpu.make_async_copy(new_own, pool.at[2 * NB], sems.at[2]),
        pltpu.make_async_copy(new_other, pool.at[2 * NB + 1], sems.at[3]),
    )
    for copy in copies:
        copy.start()
    acc[...] = jnp.zeros_like(acc)
    peak[...] = jnp.full_like(peak, LOW / 2)
    for copy in copies:
        copy.wait()

    def load(j):
        entries = pool[j]
        turned = entries.astype(F32).T
        ones = (lax.broadcasted_iota(jnp.int32, (8, BS), 0) == 0).astype(F32)
        vt[...] = jnp.concatenate([turned[HD:], ones], axis=0).astype(BF16)
        return entries[:, :HD]

    def score(keys, tile, old, mask, slot):
        scores = jnp.dot(keys, q[tile], preferred_element_type=F32)
        if mask is not None:
            scores = jnp.where(mask, scores, LOW)
        sbuf[slot] = scores
        return jnp.maximum(old, jnp.max(scores, axis=0, keepdims=True))

    def absorb(tile, old, new, slot):
        weights = jnp.exp2(sbuf[slot] - new).astype(BF16)
        keep = jnp.exp2(old - new)
        mixed = jnp.dot(vt[...], weights, preferred_element_type=F32)
        acc[tile] = acc[tile] * keep + mixed

    def sweep(keys, request, mask_of):
        olds = peak[request]
        base = request * TILES
        news = []

        def ahead(t):
            news.append(score(keys, base + t, olds[t : t + 1], mask_of(t), t % NS))

        ahead(0)
        ahead(1)
        for t in range(TILES):
            if t + 2 < TILES:
                ahead(t + 2)
            absorb(base + t, olds[t : t + 1], news[t], t % NS)
        peak[request] = jnp.concatenate(news, axis=0)

    def block(j, carry):
        request = meta[0, j]
        seen = meta[1, j]

        @pl.when(seen >= BS)
        def _():
            sweep(load(j), request, lambda t: None)

        @pl.when((seen > 0) & (seen < BS))
        def _():
            mask = lax.broadcasted_iota(jnp.int32, (BS, TOK), 0) < seen
            sweep(load(j), request, lambda t: mask)

        return carry

    lax.fori_loop(0, 2 * NB, block, 0)
    request = meta[3, 0]

    def fresh(k, carry):
        tile = meta[3, 1 + k]
        gap = lax.broadcasted_iota(jnp.int32, (BS, TOK), 0) - lax.broadcasted_iota(
            jnp.int32, (BS, TOK), 1
        )
        sweep(load(2 * NB + k), request, lambda t: gap <= (t - tile) * TOK)
        return carry

    lax.fori_loop(0, 2, fresh, 0)

    for r in range(4):
        peaks = peak[r]
        for t in range(TILES):
            state = acc[r * TILES + t]
            mass = state[HD : HD + 1]
            some = mass > 0.0
            safe = jnp.where(some, mass, 1.0)
            level = jnp.where(some, peaks[t : t + 1] + jnp.log2(safe), LOW)
            high = level.astype(BF16)
            rest = level - high.astype(F32)
            middle = rest.astype(BF16)
            low = (rest - middle.astype(F32)).astype(BF16)
            share = (state[:HD] * (1.0 / safe)).astype(BF16)
            tail = jnp.concatenate(
                [high.astype(F32), middle.astype(F32), low.astype(F32), jnp.zeros((5, TOK), F32)],
                axis=0,
            ).astype(BF16)
            out[r * TILES + t, 0:HD] = share
            out[r * TILES + t, HD:PACK] = tail


def merge_kernel(parts, w_out, out):
    heads = []
    for h in range(GROUP):
        levels = []
        for i in range(16):
            tail = parts[2 * i + h, HD:PACK].astype(F32)
            levels.append(tail[0:1] + tail[1:2] + tail[2:3])
        top = functools.reduce(jnp.maximum, levels)
        total = jnp.zeros((1, TOK), F32)
        mixed = jnp.zeros((HD, TOK), F32)
        for i in range(16):
            share = jnp.exp2(levels[i] - top)
            total = total + share
            mixed = mixed + parts[2 * i + h, 0:HD].astype(F32) * share
        heads.append(mixed / total)
    attention = jnp.concatenate(heads, axis=0).T.astype(BF16)
    out[...] = jnp.dot(attention, w_out[...], preferred_element_type=F32).astype(BF16)


def one_if(cond):
    return jnp.where(cond, 1.0, 0.0).astype(BF16)


def ranks(routes):
    experts = lax.broadcasted_iota(jnp.int32, (32, ROWS), 0)
    member = jnp.zeros((32, ROWS), F32)
    for k in range(TOP):
        member = member + jnp.where(routes[k : k + 1, :] == experts, 1.0, 0.0)
    before = one_if(
        lax.broadcasted_iota(jnp.int32, (ROWS, ROWS), 0)
        < lax.broadcasted_iota(jnp.int32, (ROWS, ROWS), 1)
    )
    rank = jnp.dot(member.astype(BF16), before, preferred_element_type=F32)
    return jnp.where(member > 0.0, rank, -1.0)


def line_slots(width):
    line = lax.broadcasted_iota(jnp.int32, (32 * LINES, width), 0) % LINES
    tail = line - 16
    slot = jnp.where(line < 16, line % 8, 8 + tail % 4)
    half = jnp.where(line < 16, line // 8, tail // 4)
    return slot.astype(F32), half


def line_experts():
    line = lax.broadcasted_iota(jnp.int32, (32 * LINES, 32), 0) // LINES
    return one_if(line == lax.broadcasted_iota(jnp.int32, (32 * LINES, 32), 1))


def dispatch_kernel(parts, hidden, gain, routes, send_out, residual_out):
    total = parts[0].astype(F32)
    for z in range(1, 8):
        total = total + parts[z].astype(F32)
    residual = (hidden[...].astype(F32) + total).astype(BF16)
    residual_out[...] = residual
    normed = rms(residual.astype(F32), gain[...])
    spread = jnp.dot(line_experts(), ranks(routes).astype(BF16), preferred_element_type=F32)
    slot, half = line_slots(ROWS)
    chosen = spread == slot
    send_out[...] = (
        jnp.dot(one_if(chosen & (half == 0)), normed[:, :512], preferred_element_type=F32)
        + jnp.dot(one_if(chosen & (half == 1)), normed[:, 512:], preferred_element_type=F32)
    ).astype(BF16)


def glu(gate, up):
    return (gate * (1.0 / (1.0 + jnp.exp(-gate))) * up).astype(BF16)


def expert_kernel(rows, w_gate, up_far, down_far, out, w_up, w_down, sems):
    up_copy = pltpu.make_async_copy(up_far.at[0], w_up, sems.at[0])
    down_copy = pltpu.make_async_copy(down_far.at[0], w_down, sems.at[1])
    up_copy.start()
    down_copy.start()
    main = jnp.concatenate(
        [rows[:, 0:8, :].reshape(256, 512), rows[:, 8:16, :].reshape(256, 512)], axis=1
    )
    tail = rows[:, 16:24, :].reshape(256, 512)

    def fold(w):
        low = jnp.dot(tail, w[:512, :], preferred_element_type=F32)
        high = jnp.dot(tail, w[512:, :], preferred_element_type=F32)
        return low + pltpu.roll(high, 252, 0)

    gate = jnp.dot(main, w_gate[...], preferred_element_type=F32)
    tail_gate = fold(w_gate)
    up_copy.wait()
    inner = glu(gate, jnp.dot(main, w_up[...], preferred_element_type=F32))
    tail_inner = glu(tail_gate, fold(w_up))
    down_copy.wait()
    answer = jnp.dot(inner, w_down[...], preferred_element_type=F32).astype(BF16)
    out[:, 0:8, :] = answer[:, :512].reshape(32, 8, 512)
    out[:, 8:16, :] = answer[:, 512:].reshape(32, 8, 512)
    answer = jnp.dot(tail_inner, w_down[...], preferred_element_type=F32)
    early = lax.broadcasted_iota(jnp.int32, (256, 512), 0) % 8 < 4
    mixed = jnp.where(early, answer[:, :512], pltpu.roll(answer[:, 512:], 4, 0))
    out[:, 16:24, :] = mixed.astype(BF16).reshape(32, 8, 512)


def settle_kernel(answers, residual, routes, gate_w, out):
    experts = lax.broadcasted_iota(jnp.int32, (32, ROWS), 0)
    gains = jnp.zeros((32, ROWS), F32)
    for k in range(TOP):
        gains = gains + jnp.where(routes[k : k + 1, :] == experts, gate_w[k : k + 1, :], 0.0)
    high = gains.astype(BF16).astype(F32)
    middle = (gains - high).astype(BF16).astype(F32)
    low = gains - high - middle
    rank = ranks(routes)
    expand = line_experts()
    places = jnp.dot(
        expand, jnp.concatenate([rank, rank, rank], axis=1).astype(BF16), preferred_element_type=F32
    )
    weights = jnp.dot(
        expand, jnp.concatenate([high, middle, low], axis=1).astype(BF16), preferred_element_type=F32
    )
    slot, half = line_slots(3 * ROWS)
    weights = jnp.where(places == slot, weights, 0.0)
    base = residual[...].astype(F32)
    for h in range(2):
        mix = jnp.where(half == h, weights, 0.0).T.astype(BF16)
        sums = jnp.dot(mix, answers[...], preferred_element_type=F32)
        total = sums[:ROWS] + sums[ROWS : 2 * ROWS] + sums[2 * ROWS :]
        columns = slice(512 * h, 512 * h + 512)
        out[:, columns] = (base[:, columns] + total).astype(BF16)


def cache_kernel(core, meta, cache, near, far, out):
    side = core[0]

    def tile_rows(i):
        return jnp.where(i % 2 == side, near[i // 2].astype(F32), far[i // 2].astype(F32))

    lane = lax.broadcasted_iota(jnp.int32, (BS, 2 * BS), 1)
    line = lax.broadcasted_iota(jnp.int32, (BS, 2 * BS), 0)
    place = lax.broadcasted_iota(jnp.int32, (BS, 2 * HD), 0)

    def block(j, carry):
        shift = meta[2, j]
        out[j] = cache[j]

        @pl.when((shift > -BS) & (shift < STRETCH))
        def _():
            base = (shift + BS) // BS - 1
            turn = shift - base * BS
            start = meta[0, j] * TILES
            left = tile_rows(start + jnp.maximum(base, 0))
            right = tile_rows(start + jnp.minimum(base + 1, TILES - 1))
            both = jnp.concatenate([left, right], axis=0).astype(BF16)
            pick = one_if(lane == line + turn)
            fresh = jnp.dot(pick, both, preferred_element_type=F32)
            inside = (place + shift >= 0) & (place + shift < STRETCH)
            out[j] = jnp.where(inside, fresh, cache[j].astype(F32)).astype(BF16)

        return carry

    lax.fori_loop(0, NB, block, 0)


def near(x):
    return pltpu.with_memory_space_constraint(x, pltpu.VMEM)


def far(x):
    return pltpu.with_memory_space_constraint(x, pltpu.HBM)


def on_device(
    hidden,
    norm1_gain,
    w_query,
    w_key,
    w_value,
    w_out,
    norm2_gain,
    w_gate,
    w_up,
    w_down,
    cache_in,
    cache_len,
    block_table,
    routes,
    gate_w,
):
    seq = lax.axis_index("seq")
    tp = lax.axis_index("tp")
    sds = jax.ShapeDtypeStruct
    swap = [(i, i ^ 1) for i in range(32)]
    cache = cache_in.reshape(NB, BS, 2 * HD)
    cache_other = lax.ppermute(cache, "seq", swap)

    request = seq // TILES
    q_send, new_rows = pl.pallas_call(
        project_kernel,
        out_shape=(sds((32, HD, TOK), BF16), sds((TOK, 2 * HD), BF16)),
        in_specs=[SM] + [VM] * 5,
        out_specs=(VM, VM),
        compiler_params=pltpu.CompilerParams(vmem_limit_bytes=8 << 20),
        name="project",
    )(cache_len, hidden, norm1_gain[None, :], w_query, w_key.T, w_value.T)
    queries = lax.all_to_all(q_send, "seq", 0, 0, tiled=True)
    rows_other = lax.ppermute(new_rows, "seq", swap)

    counts = jnp.arange(2 * NB, dtype=jnp.int32)
    ids = jnp.where(counts < NB, seq * NB + counts, (seq ^ 1) * NB + counts - NB)
    order = jnp.arange(block_table.shape[0], dtype=jnp.int32)
    slot = jnp.sum(jnp.where(block_table[None, :] == ids[:, None], order[None, :], 0), axis=1)
    block_req = slot // MAXB
    pick = block_req[:, None] == jnp.arange(4, dtype=jnp.int32)[None, :]
    block_len = jnp.sum(jnp.where(pick, cache_len[None, :], 0), axis=1)
    block_pos = slot % MAXB * BS
    shift = block_pos - block_len
    own_tile = seq % TILES
    last = jnp.where(
        counts == 0, request, jnp.where(counts == 1, own_tile, own_tile ^ 1)
    )
    meta = jnp.stack([block_req, jnp.clip(-shift, 0, BS), shift, last])

    row_send = jnp.broadcast_to(new_rows[None], (16, TOK, 2 * HD))
    queries, row_send, meta, cache_other, rows_other = lax.optimization_barrier(
        (queries, row_send, meta, cache_other, rows_other)
    )
    same_core = [[2 * chip + c for chip in range(16)] for c in range(2)]
    rows_near = lax.all_to_all(row_send, "seq", 0, 0, tiled=True, axis_index_groups=same_core)

    partial = pl.pallas_call(
        attend_kernel,
        out_shape=sds((32, PACK, TOK), BF16),
        in_specs=[SM, VM, FAR, ANY, ANY, ANY],
        out_specs=VM,
        scratch_shapes=[
            pltpu.VMEM((2 * NB + 2, BS, 2 * HD), BF16),
            pltpu.VMEM((32, PACK, TOK), F32),
            pltpu.VMEM((4, TILES, TOK), F32),
            pltpu.VMEM((PACK, BS), BF16),
            pltpu.VMEM((NS, BS, TOK), F32),
            pltpu.SemaphoreType.DMA((4,)),
        ],
        compiler_params=pltpu.CompilerParams(vmem_limit_bytes=16 << 20),
        name="attend",
    )(meta, near(queries), far(cache), far(cache_other), new_rows, rows_other)
    partial, rows_near = lax.optimization_barrier((partial, rows_near))
    parts = lax.all_to_all(partial, "seq", 0, 0, tiled=True)

    projected = pl.pallas_call(
        merge_kernel,
        out_shape=sds((TOK, D), BF16),
        in_specs=[VM, VM],
        out_specs=VM,
        compiler_params=pltpu.CompilerParams(vmem_limit_bytes=8 << 20),
        name="merge",
    )(parts, w_out)
    shares = lax.all_to_all(projected.reshape(8, ROWS, D), "tp", 0, 0, tiled=True)

    own_hidden = lax.dynamic_slice_in_dim(hidden, tp * ROWS, ROWS, 0)
    routes_t, gate_t = routes.T, gate_w.T
    send, residual = pl.pallas_call(
        dispatch_kernel,
        out_shape=(sds((32 * LINES, 512), BF16), sds((ROWS, D), BF16)),
        in_specs=[VM] * 4,
        out_specs=(VM, VM),
        compiler_params=pltpu.CompilerParams(vmem_limit_bytes=8 << 20),
        name="dispatch",
    )(near(shares), own_hidden, norm2_gain[None, :], routes_t)
    incoming = lax.all_to_all(send.reshape(32, LINES, 512), "seq", 0, 0, tiled=True)

    answer = pl.pallas_call(
        expert_kernel,
        out_shape=sds((32, LINES, 512), BF16),
        in_specs=[VM, VM, FAR, FAR],
        out_specs=VM,
        scratch_shapes=[
            pltpu.VMEM((D, FFN), BF16),
            pltpu.VMEM((FFN, D), BF16),
            pltpu.SemaphoreType.DMA((2,)),
        ],
        compiler_params=pltpu.CompilerParams(vmem_limit_bytes=20 << 20),
        name="experts",
    )(near(incoming), near(w_gate[0]), far(w_up), far(w_down))
    returned = lax.all_to_all(answer, "seq", 0, 0, tiled=True)

    hidden_out = pl.pallas_call(
        settle_kernel,
        out_shape=sds((ROWS, D), BF16),
        in_specs=[VM] * 4,
        out_specs=VM,
        compiler_params=pltpu.CompilerParams(vmem_limit_bytes=8 << 20),
        name="settle",
    )(returned.reshape(32 * LINES, 512), residual, routes_t, gate_t)

    rows_far = lax.ppermute(rows_near, "seq", swap)
    core = (seq & 1)[None]
    cache_out = pl.pallas_call(
        cache_kernel,
        out_shape=sds((NB, BS, 2 * HD), BF16),
        in_specs=[SM, SM, VM, VM, VM],
        out_specs=VM,
        compiler_params=pltpu.CompilerParams(vmem_limit_bytes=12 << 20),
        name="cache",
    )(core, meta, cache, rows_near, rows_far)
    return (hidden_out, cache_out.reshape(NB, BS, 1, 2 * HD))


def solution(mesh):
    placed = (
        P("seq", None),
        P(),
        P(None, "tp"),
        P(None, "tp"),
        P(None, "tp"),
        P("tp", None),
        P(),
        P("seq", None, None),
        P("seq", None, None),
        P("seq", None, None),
        P("seq", None, "tp", None),
        P(),
        P(),
        P(("seq", "tp"), None),
        P(("seq", "tp"), None),
    )
    return jax.shard_map(
        on_device,
        mesh=mesh,
        in_specs=placed,
        out_specs=(P(("seq", "tp"), None), P("seq", None, "tp", None)),
        check_vma=False,
    )
```
